256 devices in a mesh: cuts: 4 (over z_lo), amp: 64 (over y, x, z_hi, core).
Axes of the slice: x: 4, y: 4, z: 8 (z_hi: 2, z_lo: 4; z = z_hi * 4 + z_lo), core: 2. Of those that a mesh axis runs over, the one named last changes fastest.
Arguments:
- stem_state: bfloat16 [8, 32, 64, 128, 256], P('cuts', None, 'amp'), may hold values from -6 to 6
- gates: bfloat16 [8, 4, 2, 128, 128], P('cuts'), may hold values from -0.375 to 0.375
Outputs:
- amplitudes: float32 [32, 64, 128, 256], P('cuts', 'amp')
The draws below stay inside these ranges and needn't reach their ends.
All inputs are finite; a program needn't handle non-finite values.
Results may differ from the reference program's by a relative error of at most 0.0049.
Values may be sent and summed in bfloat16 or wider, within the bound.
No kernel may reach another device: no remote copies, remote signals or barrier semaphores. Data moves between devices by JAX's collectives and lax.ppermute only.
A program may use at most 64 MiB of HBM per device.

```python
import jax
import jax.numpy as jnp
from jax import lax

G = 128
HI = 32
SLICES = 8
N_AMP = 64


def with_spikes(values, own_key, source, target, blocks, factor):
    owner, partner = [(jnp.arange(values.shape[axis_at]) // (values.shape[axis_at] // blocks)).reshape([-1 if axis == axis_at else 1 for axis in range(values.ndim)]) for axis_at in (source, target)]
    chosen = jax.random.permutation(own_key, blocks)[partner]
    strong = (owner == chosen) | (owner == (partner + blocks // 2) % blocks)
    return jnp.where(strong, factor * values, values)


def level_of(own_key, dims, shards, low, top_value):
    factor_of = 1.0
    for axis_at, parts in shards:
        draws = jax.random.uniform(jax.random.fold_in(jax.random.fold_in(own_key, 6), axis_at), (parts,), jnp.float32, low / len(shards), top_value / len(shards))
        factor_of = factor_of * jnp.repeat(jnp.exp(draws), dims[axis_at] // parts).reshape((-1,) + (1,) * (len(dims) - 1 - axis_at))
    return factor_of


def bell_draw(key, shape, scale, bound, pieces=(), kind=jnp.bfloat16):
    values = jax.random.normal(key, shape, jnp.float32) * scale
    if len(pieces) > 0:
        values = level_of(key, shape, pieces, -0.22, 0.18) * values
    return jnp.clip(values, min=-bound, max=bound).astype(kind)


def gaussian_with(rng, extent, spread, bound, pieces, heavy, held_as=jnp.bfloat16):
    drawn = spread * jax.random.normal(rng, extent, jnp.float32)
    if pieces:
        drawn = drawn * level_of(rng, extent, pieces, -0.22, 0.18)
    return jnp.clip(with_spikes(drawn, jax.random.fold_in(rng, 3), *heavy), -bound, bound).astype(held_as)


def setup_inputs(seed: int = 0) -> dict:
    streams_of = jax.random.split(jax.random.key(seed), 3)
    stem_state = gaussian_with(streams_of[0], (SLICES, HI, N_AMP, G, 2 * G), 1.0, 6.0, ((0, 4), (2, 64)), (0, 1, 4, 2.0))
    gates = bell_draw(streams_of[1], (SLICES, 4, 2, G, G), (2 * G) ** -0.5, 0.375, ((0, 4),))
    return {"stem_state": stem_state, "gates": gates}


def block_matrix(gate):
    real_part = gate[0]
    imag_part = gate[1]
    top = jnp.concatenate([real_part.T, imag_part.T], axis=1)
    bottom = jnp.concatenate([-imag_part.T, real_part.T], axis=1)
    return jnp.concatenate([top, bottom], axis=0)


def on_rows(values, gate):
    width = values.shape[-1] // 2
    real_part = gate[0].astype(jnp.float32)
    imag_part = gate[1].astype(jnp.float32)
    first_term = jnp.einsum('ka,...ac->...kc', real_part, values.astype(jnp.float32))
    second_term = jnp.einsum('ka,...ac->...kc', imag_part, values.astype(jnp.float32))
    real_out = first_term[..., :width] - second_term[..., width:]
    imag_out = first_term[..., width:] + second_term[..., :width]
    return jnp.concatenate([real_out, imag_out], axis=-1)


def on_last(values, gate):
    columns = values.shape[-1]
    flat = values.reshape(-1, columns)
    result = jnp.dot(flat, block_matrix(gate), preferred_element_type=jnp.float32)
    return result.reshape(values.shape)


def per_value(block, gates):
    groups = block.shape[0]
    width = block.shape[1]
    low = width // groups
    first = on_rows(block, gates[0]).astype(jnp.bfloat16)
    second = on_last(first, gates[1]).astype(jnp.bfloat16)
    moved = second.reshape(groups, groups, low, 2 * width)
    moved = jnp.transpose(moved, (1, 0, 2, 3)).reshape(groups, width, 2 * width)
    third = on_rows(moved, gates[2]).astype(jnp.bfloat16)
    fourth = on_last(third, gates[3])
    back = fourth.reshape(groups, groups, low, 2 * width)
    return jnp.transpose(back, (1, 0, 2, 3)).reshape(groups, width, 2 * width)


def reference(stem_state, gates):
    def add_slice(total, pair):
        state, slice_gates = pair
        result = lax.map(lambda block: per_value(block, slice_gates), state)
        return total + result, None

    start = jnp.zeros(stem_state.shape[1:], jnp.float32)
    total, unused = lax.scan(add_slice, start, (stem_state, gates))
    return total
```

```python
import jax
import jax.numpy as jnp
from jax import lax
from jax.experimental import pallas as pl
from jax.experimental.pallas import tpu as pltpu
from jax.sharding import Mesh, PartitionSpec as P

CHUNKS = 1
PLANE = ("y", "x", "core")
COLUMN = ("zh", "cuts")
BF = jnp.bfloat16
F32 = jnp.float32


def dot(left, right):
    return jnp.dot(left, right, preferred_element_type=F32)


def dot_t(left, right):
    return lax.dot_general(left, right, (((1,), (1,)), ((), ())), preferred_element_type=F32)


def iota(shape, axis):
    return lax.broadcasted_iota(jnp.int32, shape, axis)


def select_matrix(hit):
    return jnp.where(hit, 1.0, 0.0).astype(BF)


def prepare(zh_ref, gates_ref, rows_ref, second_ref, fourth_ref, joint_ref):
    zh = zh_ref[0]
    row, col = iota((256, 128), 0), iota((256, 128), 1)
    pick = select_matrix(((row >> 3) * 4 + (row & 3)) == col)
    row_h = (row >> 2) & 1
    row, col = iota((512, 128), 0), iota((512, 128), 1)
    d, q = (row >> 3) & 31, (row >> 2) & 1
    pick_out = select_matrix((((d >> 1) * 4 + (row >> 8) * 2 + (d & 1)) * 2 + q) == col)
    row, col = iota((128, 512), 0), iota((128, 512), 1)
    d, q = col >> 4, col & 1
    pick_in = select_matrix((((d >> 1) * 4 + zh * 2 + (d & 1)) * 2 + q) == row)
    row, col = iota((512, 512), 0), iota((512, 512), 1)
    same = (row & 3) == ((col >> 1) & 3)
    col_s = (col >> 3) & 1
    for s in range(2):
        for part in range(2):
            spread = dot(pick, gates_ref[s, 0, part])
            for h2 in range(2):
                begin = part * 256 + h2 * 128
                rows_ref[s, :, begin : begin + 128] = jnp.where(row_h == h2, spread, 0.0).astype(BF)
        for layer, out in ((1, second_ref), (3, fourth_ref)):
            real, imag = gates_ref[s, layer, 0], gates_ref[s, layer, 1]
            out[s, :128, :128] = real
            out[s, :128, 128:] = -imag
            out[s, 128:, :128] = imag
            out[s, 128:, 128:] = real
    for part in range(2):
        wide = []
        for s in range(2):
            wide.append(dot(dot(pick_out, gates_ref[s, 2, part]).astype(BF), pick_in))
        mixed = jnp.where(col_s == 0, wide[0], wide[1])
        joint_ref[:, part * 512 : part * 512 + 512] = jnp.where(same, mixed, 0.0).astype(BF)


def times_i(values):
    return jnp.concatenate([-values[:, 128:], values[:, :128]], axis=1)


def before(state_ref, rows_ref, second_ref, fourth_ref, out_ref):
    pieces = []
    for s in range(2):
        state = state_ref[s, 0, 0].reshape(256, 256)
        first = dot(rows_ref[s, :, :256], state) + dot(rows_ref[s, :, 256:], times_i(state))
        second = dot_t(first.astype(BF), second_ref[s])
        pieces.append(dot_t(second.astype(BF), fourth_ref[s]).reshape(32, 8, 256))
    out_ref[:, 0] = jnp.concatenate(pieces, axis=1).astype(BF)


def after(state_ref, joint_ref, out_ref):
    state = state_ref[:, 0].reshape(512, 256)
    total = dot(joint_ref[:, :512], state) + dot(joint_ref[:, 512:], times_i(state))
    out_ref[:, 0, 0] = total.astype(BF).reshape(2, 256, 256)


def place(state_ref, out_ref):
    row, col = iota((256, 256), 0), iota((256, 256), 1)
    d, j, q, h2 = (row >> 2) & 31, (row >> 1) & 1, row & 1, row >> 7
    order = select_matrix((d * 8 + q * 4 + h2 * 2 + j) == col)
    state = state_ref[:, 0].astype(F32).reshape(256, 256).astype(BF)
    out_ref[0] = dot(order, state).reshape(2, 128, 256)


def shape_of(shape, kind=BF):
    return jax.ShapeDtypeStruct(shape, kind)


def whole(shape):
    return pl.BlockSpec(shape, lambda *at: (0,) * len(shape))


def per_device(stem_state, gates):
    chunks = CHUNKS
    pairs = 4 // chunks
    zh = lax.axis_index("zh").astype(jnp.int32).reshape(1)
    rows, second, fourth, joint = pl.pallas_call(
        prepare,
        in_specs=[pl.BlockSpec(memory_space=pltpu.SMEM), pl.BlockSpec(memory_space=pltpu.VMEM)],
        out_shape=[shape_of((2, 256, 512)), shape_of((2, 256, 256)), shape_of((2, 256, 256)), shape_of((512, 1024))],
        name="prepare",
    )(zh, gates)
    state = stem_state.reshape(2, 4, 4, 2, 128, 256)
    sums = []
    for chunk in range(chunks):
        sent = pl.pallas_call(
            before,
            grid=(pairs, 4),
            in_specs=[
                pl.BlockSpec((2, 1, 1, 2, 128, 256), lambda hp, k, c=chunk: (0, k, c * pairs + hp, 0, 0, 0)),
                whole((2, 256, 512)),
                whole((2, 256, 256)),
                whole((2, 256, 256)),
            ],
            out_specs=pl.BlockSpec((32, 1, 16, 256), lambda hp, k: (0, hp * 4 + k, 0, 0)),
            out_shape=shape_of((32, pairs * 4, 16, 256)),
            name="before",
        )(state, rows, second, fourth)
        got = lax.all_to_all(sent, PLANE, split_axis=0, concat_axis=0, tiled=True)
        partial = pl.pallas_call(
            after,
            grid=(pairs, 4),
            in_specs=[
                pl.BlockSpec((32, 1, 16, 256), lambda hp, k: (0, hp * 4 + k, 0, 0)),
                whole((512, 1024)),
            ],
            out_specs=pl.BlockSpec((2, 1, 1, 256, 256), lambda hp, k: (0, k, hp, 0, 0)),
            out_shape=shape_of((2, 4, pairs, 256, 256)),
            name="after",
        )(got, joint)
        total = lax.psum_scatter(
            partial.reshape(8, pairs * 256, 256), COLUMN, scatter_dimension=0, tiled=True
        )
        sums.append(total.reshape(pairs, 32, 8, 256))
    home = jnp.swapaxes(jnp.concatenate(sums, axis=0), 0, 1)
    home = lax.all_to_all(home, PLANE, split_axis=0, concat_axis=0, tiled=True)
    placed = pl.pallas_call(
        place,
        grid=(4,),
        in_specs=[pl.BlockSpec((32, 1, 8, 256), lambda hp: (0, hp, 0, 0))],
        out_specs=pl.BlockSpec((1, 2, 128, 256), lambda hp: (hp, 0, 0, 0)),
        out_shape=shape_of((4, 2, 128, 256), F32),
        name="place",
    )(home)
    return placed.reshape(8, 1, 128, 256)


def solution(mesh):
    fine = Mesh(mesh.devices.reshape(4, 4, 4, 2, 2), ("cuts", "y", "x", "zh", "core"))
    amp = ("y", "x", "zh", "core")
    return jax.shard_map(
        per_device,
        mesh=fine,
        in_specs=(P("cuts", None, amp, None, None), P("cuts", None, None, None, None)),
        out_specs=P("cuts", amp, None, None),
        check_vma=False,
    )
```

```python
import functools

import jax
import jax.numpy as jnp
from jax import lax
from jax.experimental import pallas as pl
from jax.experimental.pallas import tpu as pltpu
from jax.sharding import Mesh, PartitionSpec as P


CHUNKS = 2
PLANE = ("y", "x", "core")
COLUMN = ("cuts", "zh")
BF = jnp.bfloat16
F32 = jnp.float32


def dot(left, right):
    return jnp.dot(left, right, preferred_element_type=F32)


def dot_t(left, right):
    return lax.dot_general(left, right, (((1,), (1,)), ((), ())), preferred_element_type=F32)


def iota(shape, axis):
    return lax.broadcasted_iota(jnp.int32, shape, axis)


def select_matrix(hit):
    return jnp.where(hit, 1.0, 0.0).astype(BF)


def before(gates_ref, state_ref, out_ref, rows_ref, second_ref, fourth_ref):
    @pl.when(pl.program_id(0) == 0)
    def prepare():
        row, col = iota((256, 128), 0), iota((256, 128), 1)
        pick = select_matrix(((row >> 3) * 4 + (row & 3)) == col)
        row_h = (row >> 2) & 1
        for s in range(2):
            for part in range(2):
                spread = dot(pick, gates_ref[s, 0, part])
                for h2 in range(2):
                    begin = part * 256 + h2 * 128
                    rows_ref[s, :, begin : begin + 128] = jnp.where(row_h == h2, spread, 0.0).astype(BF)
            for layer, out in ((1, second_ref), (3, fourth_ref)):
                real, imag = gates_ref[s, layer, 0], gates_ref[s, layer, 1]
                out[s, :128, :128] = real
                out[s, :128, 128:] = -imag
                out[s, 128:, :128] = imag
                out[s, 128:, 128:] = real

    results = []
    for s in range(2):
        firsts = []
        for k in range(4):
            state = state_ref[s, k, 0].reshape(256, 256)
            first = dot(rows_ref[s, :, :256], state) + dot(rows_ref[s, :, 256:], times_i(state))
            firsts.append(first.astype(BF))
        second = dot_t(jnp.concatenate(firsts, axis=0), second_ref[s]).astype(BF)
        results.append(dot_t(second, fourth_ref[s]).reshape(4, 32, 8, 256))
    for k in range(4):
        out_ref[:, k] = jnp.concatenate([results[0][k], results[1][k]], axis=1).astype(BF)


def join(z_ref, gates_ref, joint_ref):
    zh = z_ref[0] >> 2
    row, col = iota((512, 128), 0), iota((512, 128), 1)
    d, q = (row >> 3) & 31, (row >> 2) & 1
    pick_out = select_matrix((((d >> 1) * 4 + (row >> 8) * 2 + (d & 1)) * 2 + q) == col)
    row, col = iota((128, 512), 0), iota((128, 512), 1)
    d, q = col >> 4, col & 1
    pick_in = select_matrix((((d >> 1) * 4 + zh * 2 + (d & 1)) * 2 + q) == row)
    row, col = iota((512, 512), 0), iota((512, 512), 1)
    same = (row & 3) == ((col >> 1) & 3)
    col_s = (col >> 3) & 1
    for part in range(2):
        wide = []
        for s in range(2):
            wide.append(dot(dot(pick_out, gates_ref[s, 2, part]).astype(BF), pick_in))
        mixed = jnp.where(col_s == 0, wide[0], wide[1])
        joint_ref[:, part * 512 : part * 512 + 512] = jnp.where(same, mixed, 0.0).astype(BF)


def times_i(values):
    return jnp.concatenate([-values[:, 128:], values[:, :128]], axis=1)


def after(way, z_ref, state_ref, joint_ref, *out_refs):
    z = z_ref[0]
    states = [state_ref[:, (z + way * step) & 3].reshape(512, 256) for step in range(4)]
    turned = [times_i(state) for state in states]
    total = dot(joint_ref[:, :512], jnp.concatenate(states, axis=1))
    total = total + dot(joint_ref[:, 512:], jnp.concatenate(turned, axis=1))
    total = total.astype(BF)
    for step in range(4):
        low, high = (total[half * 256 : half * 256 + 256, step * 256 : step * 256 + 256] for half in range(2))
        ahead = (((z + way * step) & 3) - z) & 7
        ahead = jnp.full((256, 256), ahead, jnp.int32)
        place = (way * step) & 3
        out_refs[place][0] = jnp.where(ahead < 4, low, high)
        out_refs[place + 4][0] = jnp.where(ahead < 4, high, low)


def place(state_ref, out_ref):
    row, col = iota((256, 256), 0), iota((256, 256), 1)
    d, j, q, h2 = (row >> 2) & 31, (row >> 1) & 1, row & 1, row >> 7
    order = select_matrix((d * 8 + q * 4 + h2 * 2 + j) == col)
    state = state_ref[:, 0].astype(F32).reshape(256, 256).astype(BF)
    out_ref[0] = dot(order, state).reshape(2, 128, 256)


def ring(step):
    def at(z):
        return (z % 4) * 2 + z // 4

    return [(at(z), at((z + step) % 8)) for z in range(8)]


def add(*values):
    total = values[0].astype(F32)
    for value in values[1:]:
        total = total + value.astype(F32)
    return total.astype(BF)


def reduce_column(blocks, way):
    near, far = blocks[4], blocks[-3 * way & 7]
    for step in range(1, 5):
        near = lax.ppermute(near, COLUMN, ring(way))
        if step < 4:
            near = add(near, blocks[(4 - step) * way & 7])
            far = lax.ppermute(far, COLUMN, ring(-way))
        if step < 3:
            far = add(far, blocks[(step - 3) * way & 7])
    return add(near, far, blocks[0])


def shape_of(shape, kind=BF):
    return jax.ShapeDtypeStruct(shape, kind)


def whole(shape):
    return pl.BlockSpec(shape, lambda *at: (0,) * len(shape))


def per_device_steps(stem_state, gates):
    chunks = CHUNKS
    pairs = 4 // chunks
    z = (lax.axis_index("zh") * 4 + lax.axis_index("cuts")).astype(jnp.int32).reshape(1)
    scalar = pl.BlockSpec(memory_space=pltpu.SMEM)
    joint = pl.pallas_call(
        join,
        in_specs=[scalar, pl.BlockSpec(memory_space=pltpu.VMEM)],
        out_shape=shape_of((512, 1024)),
        name="join",
    )(z, gates)
    state = stem_state.reshape(2, 4, 4, 2, 128, 256)
    sums = []
    for chunk in range(chunks):
        way = 1 - 2 * (chunk & 1)
        sent = pl.pallas_call(
            before,
            grid=(pairs,),
            in_specs=[
                whole((2, 4, 2, 128, 128)),
                pl.BlockSpec((2, 4, 1, 2, 128, 256), lambda hp, c=chunk: (0, 0, c * pairs + hp, 0, 0, 0)),
            ],
            out_specs=pl.BlockSpec((32, 4, 16, 256), lambda hp: (0, hp, 0, 0)),
            out_shape=shape_of((32, pairs * 4, 16, 256)),
            scratch_shapes=[
                pltpu.VMEM((2, 256, 512), BF),
                pltpu.VMEM((2, 256, 256), BF),
                pltpu.VMEM((2, 256, 256), BF),
            ],
            name="before",
        )(gates, state)
        got = lax.all_to_all(sent, PLANE, split_axis=0, concat_axis=0, tiled=True)
        blocks = pl.pallas_call(
            functools.partial(after, way),
            grid=(pairs,),
            in_specs=[
                scalar,
                pl.BlockSpec((32, 4, 16, 256), lambda hp: (0, hp, 0, 0)),
                whole((512, 1024)),
            ],
            out_specs=[pl.BlockSpec((1, 256, 256), lambda hp: (hp, 0, 0))] * 8,
            out_shape=[shape_of((pairs, 256, 256))] * 8,
        )(z, got, joint)
        total = reduce_column(blocks, way)
        sums.append(total.reshape(pairs, 32, 8, 256))
    home = jnp.swapaxes(jnp.concatenate(sums, axis=0), 0, 1)
    home = lax.all_to_all(home, PLANE, split_axis=0, concat_axis=0, tiled=True)
    placed = pl.pallas_call(
        place,
        grid=(4,),
        in_specs=[pl.BlockSpec((32, 1, 8, 256), lambda hp: (0, hp, 0, 0))],
        out_specs=pl.BlockSpec((1, 2, 128, 256), lambda hp: (hp, 0, 0, 0)),
        out_shape=shape_of((4, 2, 128, 256), F32),
        name="place",
    )(home)
    return placed.reshape(8, 1, 128, 256)


def solution(mesh):
    fine = Mesh(mesh.devices.reshape(4, 4, 4, 2, 2), ("cuts", "y", "x", "zh", "core"))
    amp = ("y", "x", "zh", "core")
    return jax.shard_map(
        per_device_steps,
        mesh=fine,
        in_specs=(P("cuts", None, amp, None, None), P("cuts", None, None, None, None)),
        out_specs=P("cuts", amp, None, None),
        check_vma=False,
    )
```

```python
import functools

import jax
import jax.numpy as jnp
from jax import lax
from jax.experimental import pallas as pl
from jax.experimental.pallas import tpu as pltpu
from jax.sharding import Mesh, PartitionSpec as P


SIZES = (2, 2)
PLANE = ("y", "x", "core")
COLUMN = ("cuts", "zh")
BF = jnp.bfloat16
F32 = jnp.float32
LIMIT = pltpu.CompilerParams(vmem_limit_bytes=16 << 20)


def dot(left, right):
    return jnp.dot(left, right, preferred_element_type=F32)


def dot_t(left, right):
    return lax.dot_general(left, right, (((1,), (1,)), ((), ())), preferred_element_type=F32)


def iota(shape, axis):
    return lax.broadcasted_iota(jnp.int32, shape, axis)


def select_matrix(hit):
    return jnp.where(hit, 1.0, 0.0).astype(BF)


def before(gates_ref, state_ref, out_ref, rows_ref, second_ref, fourth_ref):
    @pl.when(pl.program_id(0) == 0)
    def prepare():
        row, col = iota((256, 128), 0), iota((256, 128), 1)
        pick = select_matrix(((row >> 3) * 4 + (row & 3)) == col)
        row_h = (row >> 2) & 1
        for s in range(2):
            for part in range(2):
                spread = dot(pick, gates_ref[s, 0, part])
                for h2 in range(2):
                    begin = part * 256 + h2 * 128
                    rows_ref[s, :, begin : begin + 128] = jnp.where(row_h == h2, spread, 0.0).astype(BF)
            for layer, out in ((1, second_ref), (3, fourth_ref)):
                real, imag = gates_ref[s, layer, 0], gates_ref[s, layer, 1]
                out[s, :128, :128] = real
                out[s, :128, 128:] = -imag
                out[s, 128:, :128] = imag
                out[s, 128:, 128:] = real

    results = []
    for s in range(2):
        firsts = []
        for k in range(4):
            state = state_ref[s, k, 0].reshape(256, 256)
            first = dot(rows_ref[s, :, :256], state) + dot(rows_ref[s, :, 256:], times_i(state))
            firsts.append(first.astype(BF))
        second = dot_t(jnp.concatenate(firsts, axis=0), second_ref[s]).astype(BF)
        results.append(dot_t(second, fourth_ref[s]).reshape(4, 32, 8, 256))
    for k in range(4):
        out_ref[:, k] = jnp.concatenate([results[0][k], results[1][k]], axis=1).astype(BF)


def join(z_ref, gates_ref, joint_ref):
    zh = z_ref[0] >> 2
    row, col = iota((512, 128), 0), iota((512, 128), 1)
    d, q = (row >> 3) & 31, (row >> 2) & 1
    pick_out = select_matrix((((d >> 1) * 4 + (row >> 8) * 2 + (d & 1)) * 2 + q) == col)
    row, col = iota((128, 512), 0), iota((128, 512), 1)
    d, q = col >> 4, col & 1
    pick_in = select_matrix((((d >> 1) * 4 + zh * 2 + (d & 1)) * 2 + q) == row)
    row, col = iota((512, 512), 0), iota((512, 512), 1)
    same = (row & 3) == ((col >> 1) & 3)
    col_s = (col >> 3) & 1
    for part in range(2):
        wide = []
        for s in range(2):
            wide.append(dot(dot(pick_out, gates_ref[s, 2, part]).astype(BF), pick_in))
        mixed = jnp.where(col_s == 0, wide[0], wide[1])
        joint_ref[:, part * 512 : part * 512 + 512] = jnp.where(same, mixed, 0.0).astype(BF)


def times_i(values):
    return jnp.concatenate([-values[:, 128:], values[:, :128]], axis=1)


def after(way, z_ref, state_ref, joint_ref, *out_refs):
    z = z_ref[0]
    states = [state_ref[:, (z + way * step) & 3].reshape(512, 256) for step in range(4)]
    turned = [times_i(state) for state in states]
    total = dot(joint_ref[:, :512], jnp.concatenate(states, axis=1))
    total = total + dot(joint_ref[:, 512:], jnp.concatenate(turned, axis=1))
    total = total.astype(BF)
    first = (4, 2 * way & 7)
    rest = [place for place in range(8) if place not in first]

    def put(place, value):
        if place in first:
            out_refs[0][first.index(place)] = value
        else:
            out_refs[1 + rest.index(place)][...] = value

    for step in range(4):
        low, high = (total[half * 256 : half * 256 + 256, step * 256 : step * 256 + 256] for half in range(2))
        ahead = (((z + way * step) & 3) - z) & 7
        ahead = jnp.full((256, 256), ahead, jnp.int32)
        place = (way * step) & 3
        put(place, jnp.where(ahead < 4, low, high))
        put(place + 4, jnp.where(ahead < 4, high, low))


def place(state_ref, out_ref):
    row, col = iota((256, 256), 0), iota((256, 256), 1)
    d, j, q, h2 = (row >> 2) & 31, (row >> 1) & 1, row & 1, row >> 7
    order = select_matrix((d * 8 + q * 4 + h2 * 2 + j) == col)
    for part in range(2):
        state = state_ref[:, pl.program_id(0) * 2 + part].astype(F32).reshape(256, 256).astype(BF)
        out_ref[part] = dot(order, state).reshape(2, 128, 256)


def ring(step):
    def at(z):
        return (z % 4) * 2 + z // 4

    return [(at(z), at((z + step) % 8)) for z in range(8)]


def add(*values):
    total = values[0].astype(F32)
    for value in values[1:]:
        total = total + value.astype(F32)
    return total.astype(BF)


def reduce_column(arrays, way):
    pair = arrays[0]
    rest = [place for place in range(8) if place not in (4, 2 * way & 7)]
    blocks = {place: array for place, array in zip(rest, arrays[1:])}

    def own(ahead):
        return blocks[ahead * way & 7]

    def shift(value, step):
        return lax.ppermute(value, COLUMN, ring(step * way))

    pair, far = shift(pair, 1), shift(own(-3), -1)
    near, far = add(pair[0], own(3)), add(far, own(-2))
    near, far = shift(near, 2), shift(far, -1)
    near, far = add(near, pair[1], own(1)), add(far, own(-1))
    near, far = shift(near, 1), shift(far, -1)
    return add(near, far, own(0))


def shape_of(shape, kind=BF):
    return jax.ShapeDtypeStruct(shape, kind)


def whole(shape):
    return pl.BlockSpec(shape, lambda *at: (0,) * len(shape))


def per_device_steps(stem_state, gates):
    z = (lax.axis_index("zh") * 4 + lax.axis_index("cuts")).astype(jnp.int32).reshape(1)
    scalar = pl.BlockSpec(memory_space=pltpu.SMEM)
    local = pl.BlockSpec(memory_space=pltpu.VMEM)
    joint = pl.pallas_call(
        join,
        in_specs=[scalar, local],
        out_specs=local,
        out_shape=pltpu.VMEM((512, 1024), BF),
        compiler_params=LIMIT,
        name="join",
    )(z, gates)
    state = stem_state.reshape(2, 4, 4, 2, 128, 256)
    sums = []
    for chunk, pairs in enumerate(SIZES):
        begin = sum(SIZES[:chunk])
        sent = pl.pallas_call(
            before,
            grid=(pairs,),
            in_specs=[
                whole((2, 4, 2, 128, 128)),
                pl.BlockSpec((2, 4, 1, 2, 128, 256), lambda hp, begin=begin: (0, 0, begin + hp, 0, 0, 0)),
            ],
            out_specs=pl.BlockSpec((32, 4, 16, 256), lambda hp: (0, hp, 0, 0)),
            out_shape=shape_of((32, pairs * 4, 16, 256)),
            scratch_shapes=[
                pltpu.VMEM((2, 256, 512), BF),
                pltpu.VMEM((2, 256, 256), BF),
                pltpu.VMEM((2, 256, 256), BF),
            ],
            name="before",
        )(gates, state)
        got = lax.all_to_all(sent, PLANE, split_axis=0, concat_axis=0, tiled=True)
        if chunk == 0:
            got = pltpu.with_memory_space_constraint(got, pltpu.HBM)
        for pair in range(pairs):
            way = 1 - 2 * (pair & 1)
            blocks = pl.pallas_call(
                functools.partial(after, way),
                grid=(1,),
                in_specs=[scalar, pl.BlockSpec((32, 4, 16, 256), lambda i, pair=pair: (0, pair, 0, 0)), local],
                out_specs=[local] * 7,
                out_shape=[pltpu.VMEM((2, 256, 256), BF)] + [pltpu.VMEM((256, 256), BF)] * 6,
                compiler_params=LIMIT,
            )(z, got, joint)
            total = reduce_column(blocks, way)
            sums.append(total.reshape(1, 32, 8, 256))
    home = jnp.swapaxes(jnp.concatenate(sums, axis=0), 0, 1)
    home = lax.all_to_all(home, PLANE, split_axis=0, concat_axis=0, tiled=True)
    placed = pl.pallas_call(
        place,
        grid=(2,),
        in_specs=[local],
        out_specs=pl.BlockSpec((2, 2, 128, 256), lambda step: (step, 0, 0, 0)),
        out_shape=shape_of((4, 2, 128, 256), F32),
        compiler_params=LIMIT,
        name="place",
    )(home)
    return placed.reshape(8, 1, 128, 256)


def solution(mesh):
    fine = Mesh(mesh.devices.reshape(4, 4, 4, 2, 2), ("cuts", "y", "x", "zh", "core"))
    amp = ("y", "x", "zh", "core")
    return jax.shard_map(
        per_device_steps,
        mesh=fine,
        in_specs=(P("cuts", None, amp, None, None), P("cuts", None, None, None, None)),
        out_specs=P("cuts", amp, None, None),
        check_vma=False,
    )
```

```python
import functools

import jax
import jax.numpy as jnp
from jax import lax
from jax.experimental import pallas as pl
from jax.experimental.pallas import tpu as pltpu
from jax.sharding import Mesh, PartitionSpec as P


CHUNKS = 2
PLANE = ("y", "x", "core")
COLUMN = ("cuts", "zh")
BF = jnp.bfloat16
F32 = jnp.float32
LIMIT = pltpu.CompilerParams(vmem_limit_bytes=16 << 20)


def dot(left, right):
    return jnp.dot(left, right, preferred_element_type=F32)


def dot_t(left, right):
    return lax.dot_general(left, right, (((1,), (1,)), ((), ())), preferred_element_type=F32)


def iota(shape, axis):
    return lax.broadcasted_iota(jnp.int32, shape, axis)


def select_matrix(hit):
    return jnp.where(hit, 1.0, 0.0).astype(BF)


def before(gates_ref, state_ref, out_ref, rows_ref, second_ref, fourth_ref):
    @pl.when(pl.program_id(0) == 0)
    def prepare():
        row, col = iota((256, 128), 0), iota((256, 128), 1)
        pick = select_matrix(((row >> 3) * 4 + (row & 3)) == col)
        row_h = (row >> 2) & 1
        for s in range(2):
            for part in range(2):
                spread = dot(pick, gates_ref[s, 0, part])
                for h2 in range(2):
                    begin = part * 256 + h2 * 128
                    rows_ref[s, :, begin : begin + 128] = jnp.where(row_h == h2, spread, 0.0).astype(BF)
            for layer, out in ((1, second_ref), (3, fourth_ref)):
                real, imag = gates_ref[s, layer, 0], gates_ref[s, layer, 1]
                out[s, :128, :128] = real
                out[s, :128, 128:] = -imag
                out[s, 128:, :128] = imag
                out[s, 128:, 128:] = real

    results = []
    for s in range(2):
        firsts = []
        for k in range(4):
            state = state_ref[s, k, 0].reshape(256, 256)
            first = dot(rows_ref[s, :, :256], state) + dot(rows_ref[s, :, 256:], times_i(state))
            firsts.append(first.astype(BF))
        second = dot_t(jnp.concatenate(firsts, axis=0), second_ref[s]).astype(BF)
        results.append(dot_t(second, fourth_ref[s]).reshape(4, 32, 8, 256))
    for k in range(4):
        out_ref[:, k] = jnp.concatenate([results[0][k], results[1][k]], axis=1).astype(BF)


def join(z_ref, gates_ref, joint_ref):
    zh = z_ref[0] >> 2
    row, col = iota((512, 128), 0), iota((512, 128), 1)
    d, q = (row >> 3) & 31, (row >> 2) & 1
    pick_out = select_matrix((((d >> 1) * 4 + (row >> 8) * 2 + (d & 1)) * 2 + q) == col)
    row, col = iota((128, 512), 0), iota((128, 512), 1)
    d, q = col >> 4, col & 1
    pick_in = select_matrix((((d >> 1) * 4 + zh * 2 + (d & 1)) * 2 + q) == row)
    row, col = iota((512, 512), 0), iota((512, 512), 1)
    same = (row & 3) == ((col >> 1) & 3)
    col_s = (col >> 3) & 1
    for part in range(2):
        wide = []
        for s in range(2):
            wide.append(dot(dot(pick_out, gates_ref[s, 2, part]).astype(BF), pick_in))
        mixed = jnp.where(col_s == 0, wide[0], wide[1])
        joint_ref[:, part * 512 : part * 512 + 512] = jnp.where(same, mixed, 0.0).astype(BF)


def times_i(values):
    return jnp.concatenate([-values[:, 128:], values[:, :128]], axis=1)


def after(way, z_ref, state_ref, joint_ref, *out_refs):
    z = z_ref[0]
    states = [state_ref[:, (z + way * step) & 3].reshape(512, 256) for step in range(4)]
    turned = [times_i(state) for state in states]
    total = dot(joint_ref[:, :512], jnp.concatenate(states, axis=1))
    total = total + dot(joint_ref[:, 512:], jnp.concatenate(turned, axis=1))
    total = total.astype(BF)
    for step in range(4):
        low, high = (total[half * 256 : half * 256 + 256, step * 256 : step * 256 + 256] for half in range(2))
        ahead = (((z + way * step) & 3) - z) & 7
        ahead = jnp.full((256, 256), ahead, jnp.int32)
        place = (way * step) & 3
        out_refs[place][...] = jnp.where(ahead < 4, low, high)
        out_refs[place + 4][...] = jnp.where(ahead < 4, high, low)


def place(state_ref, out_ref):
    row, col = iota((256, 256), 0), iota((256, 256), 1)
    d, j, q, h2 = (row >> 2) & 31, (row >> 1) & 1, row & 1, row >> 7
    order = select_matrix((d * 8 + q * 4 + h2 * 2 + j) == col)
    for part in range(2):
        state = state_ref[:, pl.program_id(0) * 2 + part].astype(F32).reshape(256, 256).astype(BF)
        out_ref[part] = dot(order, state).reshape(2, 128, 256)


def ring(step):
    def at(z):
        return (z % 4) * 2 + z // 4

    return [(at(z), at((z + step) % 8)) for z in range(8)]


def add(*values):
    total = values[0].astype(F32)
    for value in values[1:]:
        total = total + value.astype(F32)
    return total.astype(BF)


def reduce_column(blocks, way):
    near, far = blocks[4], blocks[-3 * way & 7]
    for step in range(1, 5):
        near = lax.ppermute(near, COLUMN, ring(way))
        if step < 4:
            near = add(near, blocks[(4 - step) * way & 7])
            far = lax.ppermute(far, COLUMN, ring(-way))
        if step < 3:
            far = add(far, blocks[(step - 3) * way & 7])
    return add(near, far, blocks[0])


def shape_of(shape, kind=BF):
    return jax.ShapeDtypeStruct(shape, kind)


def whole(shape):
    return pl.BlockSpec(shape, lambda *at: (0,) * len(shape))


def per_device_steps(stem_state, gates):
    chunks = CHUNKS
    pairs = 4 // chunks
    z = (lax.axis_index("zh") * 4 + lax.axis_index("cuts")).astype(jnp.int32).reshape(1)
    scalar = pl.BlockSpec(memory_space=pltpu.SMEM)
    local = pl.BlockSpec(memory_space=pltpu.VMEM)
    joint = pl.pallas_call(
        join,
        in_specs=[scalar, local],
        out_specs=local,
        out_shape=pltpu.VMEM((512, 1024), BF),
        compiler_params=LIMIT,
        name="join",
    )(z, gates)
    state = stem_state.reshape(2, 4, 4, 2, 128, 256)
    sums = []
    for chunk in range(chunks):
        sent = pl.pallas_call(
            before,
            grid=(pairs,),
            in_specs=[
                whole((2, 4, 2, 128, 128)),
                pl.BlockSpec((2, 4, 1, 2, 128, 256), lambda hp, c=chunk: (0, 0, c * pairs + hp, 0, 0, 0)),
            ],
            out_specs=pl.BlockSpec((32, 4, 16, 256), lambda hp: (0, hp, 0, 0)),
            out_shape=shape_of((32, pairs * 4, 16, 256)),
            scratch_shapes=[
                pltpu.VMEM((2, 256, 512), BF),
                pltpu.VMEM((2, 256, 256), BF),
                pltpu.VMEM((2, 256, 256), BF),
            ],
            name="before",
        )(gates, state)
        got = lax.all_to_all(sent, PLANE, split_axis=0, concat_axis=0, tiled=True)
        if chunk == 0:
            got = pltpu.with_memory_space_constraint(got, pltpu.HBM)
        for pair in range(pairs):
            way = 1 - 2 * (pair & 1)
            blocks = pl.pallas_call(
                functools.partial(after, way),
                grid=(1,),
                in_specs=[scalar, pl.BlockSpec((32, 4, 16, 256), lambda i, pair=pair: (0, pair, 0, 0)), local],
                out_specs=[local] * 8,
                out_shape=[pltpu.VMEM((256, 256), BF)] * 8,
                compiler_params=LIMIT,
            )(z, got, joint)
            total = reduce_column(blocks, way)
            sums.append(total.reshape(1, 32, 8, 256))
    home = jnp.swapaxes(jnp.concatenate(sums, axis=0), 0, 1)
    home = lax.all_to_all(home, PLANE, split_axis=0, concat_axis=0, tiled=True)
    placed = pl.pallas_call(
        place,
        grid=(2,),
        in_specs=[local],
        out_specs=pl.BlockSpec((2, 2, 128, 256), lambda step: (step, 0, 0, 0)),
        out_shape=shape_of((4, 2, 128, 256), F32),
        compiler_params=LIMIT,
        name="place",
    )(home)
    return placed.reshape(8, 1, 128, 256)


def solution(mesh):
    fine = Mesh(mesh.devices.reshape(4, 4, 4, 2, 2), ("cuts", "y", "x", "zh", "core"))
    amp = ("y", "x", "zh", "core")
    return jax.shard_map(
        per_device_steps,
        mesh=fine,
        in_specs=(P("cuts", None, amp, None, None), P("cuts", None, None, None, None)),
        out_specs=P("cuts", amp, None, None),
        check_vma=False,
    )
```
